256 devices in a mesh: rows: 64 (over y, z, core), cols: 4 (over x).
Axes of the slice: x: 4, y: 4, z: 8, core: 2. Of those that a mesh axis runs over, the one named last changes fastest.
Arguments:
- inner_pivots: float32 [3072, 128, 128], P(('rows', 'cols')), may hold values from 0 to 4, as said below
- lower_blocks: float32 [3072, 4, 128, 128], P('rows', 'cols'), may hold values from -0.13 to 0.13
- upper_blocks: float32 [3072, 4, 128, 128], P('rows', 'cols'), may hold values from -0.13 to 0.13
- separator_pivots: float32 [64, 128, 128], P('rows', 'cols'), may hold values from 0 to 16, as said below
- separator_ids: int32 [3072, 4], P('rows', 'cols'), may hold values from 0 to 63, all different within a row
- coupling_count: int32 [3072], P('rows'), may hold values from 1 to 4
Outputs:
- inner_inverse: float32 [3072, 128, 128], P(('rows', 'cols'))
- lower_factor: float32 [3072, 4, 128, 128], P('rows', 'cols')
- separator_inverse: float32 [64, 128, 128], P('rows', 'cols')
The draws below stay inside these ranges and needn't reach their ends.
Inputs may be any that keep to these rules, and one draw needn't show every extreme that they name: `inner_pivots`: each row's diagonal entry is positive and larger than the sum of the magnitudes of the row's other entries. `separator_pivots`: each row's diagonal entry is positive and larger than the sum of the magnitudes of the row's other entries. `separator_ids`: the 4 slots of an interior name different separators; every separator is named by some slot. Interior i couples through its first coupling_count[i] slots only.
All inputs are finite; a program needn't handle non-finite values.
Results may differ from the reference program's by a relative error of at most 0.0001.
Values sent between devices are 32-bit elements; how exact they have to be, the bound alone decides.
A program may use at most 64 MiB of HBM per device.

```python
import math
import jax
import jax.numpy as jnp
from jax import lax

B = 128
INT_DEV = 12
W = 32
K = 4
NINT = 3072
NSEP = 64
N_ROWS = 64
N_COLS = 4


def banded_pivots(scales, weights):
    reach = max(B // 16, 2)
    positions = jnp.arange(B, dtype=jnp.float32)
    distance = jnp.abs(positions[:, None] - positions[None, :])
    identity = jnp.eye(B, dtype=jnp.float32)
    kernel = jnp.exp(-distance / reach) * (1.0 - identity)
    factor = 0.95 * (math.exp(1.0 / reach) - 1.0) / 2.0
    spread_part = scales[:, :, None] * factor * weights * kernel[None, :, :]
    return spread_part + identity * scales[:, :, None]


def draw_inner_pivots(key, part):
    first_key, second_key = jax.random.split(jax.random.fold_in(key, 11))
    weights = jax.random.uniform(first_key, (NINT, B, B), jnp.float32, 0.8, 1.0)
    scales = jnp.exp(jax.random.uniform(second_key, (NINT, B), jnp.float32, 0.0, math.log(4.0)))
    return banded_pivots(scales, weights)


def draw_separator_pivots(key, part):
    first_key, second_key = jax.random.split(jax.random.fold_in(key, 23))
    weights = jax.random.uniform(first_key, (NSEP, B, B), jnp.float32, 0.8, 1.0)
    scales = jnp.exp(jax.random.uniform(second_key, (NSEP, B), jnp.float32, math.log(6.0), math.log(16.0)))
    return banded_pivots(scales, weights)


def with_ends(entries, own_key, smallest, top_value):
    spot = [jax.random.randint(jax.random.fold_in(own_key, axis), (), 0, length) for axis, length in enumerate(entries.shape)]
    longest = entries.shape.index(max(entries.shape))
    neighbour = spot[:longest] + [(spot[longest] + 1) % entries.shape[longest]] + spot[longest + 1:]
    return entries.at[tuple(spot)].set(smallest).at[tuple(neighbour)].set(top_value)


def level_of(key, dims, cuts, least, top_value):
    factor_of, own = 1.0, jax.random.fold_in(key, 6)
    for axis_at, parts in cuts:
        heights = jnp.exp(jax.random.uniform(jax.random.fold_in(own, axis_at), (parts,), jnp.float32, least / len(cuts), top_value / len(cuts)))
        factor_of = factor_of * jnp.repeat(heights, dims[axis_at] // parts).reshape([-1 if axis == axis_at else 1 for axis in range(len(dims))])
    return factor_of


def picks_of(own_key, rows, number_of, top, lift):
    ranking = jax.random.permutation(jax.random.fold_in(own_key, 1), number_of)
    pull = ranking
    for power in range(3):
        pull = pull * pull // number_of
    pull = pull * lift // number_of
    chance = jax.random.randint(jax.random.fold_in(own_key, 2), (rows, number_of), 0, 4096) + pull
    fixed_rows = jax.random.permutation(jax.random.fold_in(own_key, 3), rows)[jnp.arange(number_of) % rows]
    chance = jnp.where(jnp.arange(rows)[:, None] == fixed_rows[None, :], 1 << 14, chance)
    score = chance * number_of + jnp.arange(number_of)
    return lax.top_k(score.astype(jnp.int32), top)[1].astype(jnp.int32)


def centred(stream_key, extent, scale, most, cuts=(), held_as=jnp.bfloat16):
    array = scale * jax.random.normal(stream_key, extent, jnp.float32)
    if cuts:
        array = array * level_of(stream_key, extent, cuts, -0.22, 0.18)
    return jnp.clip(array, -most, most).astype(held_as)


def setup_inputs(seed: int = 0) -> dict:
    arg_keys = jax.random.split(jax.random.key(seed), 7)
    return {
        "inner_pivots": draw_inner_pivots(jax.random.fold_in(arg_keys[6], 71), 0),
        "lower_blocks": centred(arg_keys[1], (NINT, K, B, B), 0.022, 0.13, ((0, 64), (1, 4)), jnp.float32),
        "upper_blocks": centred(arg_keys[2], (NINT, K, B, B), 0.022, 0.13, ((0, 64), (1, 4)), jnp.float32),
        "separator_pivots": draw_separator_pivots(jax.random.fold_in(arg_keys[6], 71), 0),
        "separator_ids": picks_of(arg_keys[4], NINT, NSEP, K, 512),
        "coupling_count": with_ends(jax.random.randint(arg_keys[5], (NINT,), 1, K + 1), jax.random.fold_in(arg_keys[5], 1), 1, K).astype(jnp.int32),
    }


HIGHEST = lax.Precision.HIGHEST


def small_inverse(block):
    width = block.shape[1]
    identity = jnp.broadcast_to(jnp.eye(width, dtype=block.dtype), block.shape)
    augmented = jnp.concatenate([block, identity], axis=2)

    def eliminate(step_index, augmented):
        position = step_index.astype(jnp.int32)
        pivot_row = lax.dynamic_slice_in_dim(augmented, position, 1, 1)
        pivot_value = lax.dynamic_slice_in_dim(pivot_row, position, 1, 2)
        pivot_row = pivot_row / pivot_value
        pivot_column = lax.dynamic_slice_in_dim(augmented, position, 1, 2)
        augmented = augmented - pivot_column * pivot_row
        return lax.dynamic_update_slice_in_dim(augmented, pivot_row, position, 1)

    augmented = lax.fori_loop(0, width, eliminate, augmented)
    return augmented[:, :, width:]


def blocked_inverse(matrix, panel_width):
    block_size = matrix.shape[1]
    identity = jnp.broadcast_to(jnp.eye(block_size, dtype=matrix.dtype), matrix.shape)
    augmented = jnp.concatenate([matrix, identity], axis=2)
    for panel in range(block_size // panel_width):
        offset = panel * panel_width
        pivot_rows = augmented[:, offset:offset + panel_width, :]
        pivot_inv = small_inverse(pivot_rows[:, :, offset:offset + panel_width])
        scaled = jnp.einsum("nij,njc->nic", pivot_inv, pivot_rows, precision=HIGHEST)
        panel_columns = augmented[:, :, offset:offset + panel_width]
        augmented = augmented - jnp.einsum("nij,njc->nic", panel_columns, scaled, precision=HIGHEST)
        augmented = augmented.at[:, offset:offset + panel_width, :].set(scaled)
    return augmented[:, :, block_size:]


def reference(inner_pivots, lower_blocks, upper_blocks, separator_pivots, separator_ids, coupling_count):
    inner_inverse = blocked_inverse(inner_pivots, W)
    slot_ids = jnp.arange(K, dtype=jnp.int32)
    live_slots = slot_ids[None, :] < coupling_count[:, None]
    group_rows = INT_DEV * N_COLS
    stacked = (
        lower_blocks.reshape(N_ROWS, group_rows, K, B, B),
        upper_blocks.reshape(N_ROWS, group_rows, K, B, B),
        inner_inverse.reshape(N_ROWS, group_rows, B, B),
        separator_ids.reshape(N_ROWS, group_rows, K),
        live_slots.reshape(N_ROWS, group_rows, K),
    )

    def accumulate(running, pieces):
        lower_part, upper_part, inverse_part, id_part, live_part = pieces
        factor = jnp.einsum("ikab,ibc->ikac", lower_part, inverse_part, precision=HIGHEST)
        factor = jnp.where(live_part[:, :, None, None], factor, jnp.zeros_like(factor))
        product = jnp.einsum("ikab,ikbc->ikac", factor, upper_part, precision=HIGHEST)
        running = running + jax.ops.segment_sum(product.reshape(-1, B, B), id_part.reshape(-1), num_segments=NSEP)
        return running, factor

    initial = jnp.zeros((NSEP, B, B), separator_pivots.dtype)
    schur_sum, lower_factor = lax.scan(accumulate, initial, stacked)
    separator_inverse = blocked_inverse(separator_pivots - schur_sum, W)
    return inner_inverse, lower_factor.reshape(NINT, K, B, B), separator_inverse
```

```python
import functools

import jax
import jax.numpy as jnp
from jax import lax
from jax.experimental import pallas as pl
from jax.experimental.pallas import tpu as pltpu
from jax.sharding import PartitionSpec as P

HIGH = lax.Precision.HIGH
VMEM = pl.BlockSpec(memory_space=pltpu.VMEM)
SMEM = pl.BlockSpec(memory_space=pltpu.SMEM)
GRANT = 48 << 20


def dot(a, b):
    return lax.dot_general(a, b, (((1,), (0,)), ((), ())), precision=HIGH, preferred_element_type=jnp.float32)


def eliminate(slabs, first, ahead):
    depth, width = slabs[0].shape
    lanes = lax.broadcasted_iota(jnp.int32, (1, width), 1)
    rows = lax.broadcasted_iota(jnp.int32, (depth, width), 0)
    for start in range(0, depth, ahead):
        base = first + start
        spread = [
            [jnp.broadcast_to(slab[:, base + t : base + t + 1], (depth, width)) for t in range(ahead)]
            for slab in slabs
        ]
        for t in range(ahead):
            k = start + t
            at_lane = (lanes == base + t).astype(jnp.float32)
            at_row = (rows == k).astype(jnp.float32)
            for index, slab in enumerate(slabs):
                columns = spread[index]
                inverse = 1.0 / columns[t][k : k + 1, :]
                pivot_row = (slab[k : k + 1, :] + at_lane) * inverse
                column = columns[t] - at_row
                for u in range(t + 1, ahead):
                    columns[u] = columns[u] - column * (columns[u][k : k + 1, :] * inverse)
                slabs[index] = slab - column * pivot_row
    return slabs


def invert(ref, members, panel, ahead):
    size = ref.shape[-1]
    lanes = lax.broadcasted_iota(jnp.int32, (1, size), 1)
    for first in range(0, size, panel):
        slabs = eliminate([ref[b, first : first + panel, :] for b in members], first, ahead)
        inside = (lanes >= first) & (lanes < first + panel)
        for b, slab in zip(members, slabs):
            whole = ref[b]
            update = dot(whole[:, first : first + panel], slab)
            ref[b] = jnp.where(inside, 0.0, whole) - update
            ref[b, first : first + panel, :] = slab


def interiors_kernel(pivots, out):
    out[...] = pivots[...]
    invert(out, range(pivots.shape[0]), 8, 8)


def couplings_kernel(group, first_slot, ids, counts, inverses, lower, upper, factor, schur):
    step = pl.program_id(0)

    @pl.when(step == 0)
    def _():
        schur[...] = jnp.zeros_like(schur)

    products = []
    for g in range(group):
        live = first_slot[0] < counts[step * group + g]
        value = jnp.where(live, dot(lower[g, 0], inverses[g]), 0.0)
        factor[g, 0] = value
        products.append(dot(value, upper[g, 0]))
    for g in range(group):
        j = ids[step * group + g]
        schur[j] = schur[j] + products[g]


def separator_kernel(pivots, total, own, out, work):
    work[0] = pivots[...] - total[...]
    invert(work, range(1), 32, 16)
    rows = out.shape[0]
    out[...] = work[0, pl.ds(pl.multiple_of(own[0] * rows, rows), rows), :]


def shards(inner_pivots, lower_blocks, upper_blocks, separator_pivots, separator_ids, coupling_count):
    f32 = jnp.float32
    count, size = inner_pivots.shape[0], inner_pivots.shape[1]
    couplings = lower_blocks.shape[0]
    col = lax.axis_index("cols").astype(jnp.int32)
    separators = separator_pivots.shape[0] * lax.axis_size("rows")
    params = pltpu.CompilerParams(vmem_limit_bytes=GRANT)

    inner_inverse = pl.pallas_call(
        interiors_kernel,
        out_shape=jax.ShapeDtypeStruct((count, size, size), f32),
        in_specs=[VMEM],
        out_specs=VMEM,
        compiler_params=params,
    )(inner_pivots)
    inverses = lax.all_gather(inner_inverse, "cols", axis=0, tiled=True)

    group = 6
    block = pl.BlockSpec((group, 1, size, size), lambda s, *_: (s, 0, 0, 0))
    lower_factor, schur = pl.pallas_call(
        functools.partial(couplings_kernel, group),
        grid_spec=pltpu.PrefetchScalarGridSpec(
            num_scalar_prefetch=3,
            grid=(couplings // group,),
            in_specs=[pl.BlockSpec((group, size, size), lambda s, *_: (s, 0, 0)), block, block],
            out_specs=[block, pl.BlockSpec((separators, size, size), lambda s, *_: (0, 0, 0))],
        ),
        out_shape=[
            jax.ShapeDtypeStruct(lower_blocks.shape, f32),
            jax.ShapeDtypeStruct((separators, size, size), f32),
        ],
        compiler_params=params,
    )(col[None], separator_ids.reshape(-1), coupling_count, inverses, lower_blocks, upper_blocks)

    summed = lax.psum_scatter(schur, "rows", scatter_dimension=0, tiled=True)
    summed = lax.psum(summed, "cols")
    pivots = lax.all_gather(separator_pivots, "cols", axis=1, tiled=True)
    own = pl.pallas_call(
        separator_kernel,
        out_shape=jax.ShapeDtypeStruct(separator_pivots.shape[1:], f32),
        in_specs=[VMEM, VMEM, SMEM],
        out_specs=VMEM,
        scratch_shapes=[pltpu.VMEM((1, size, size), f32)],
        compiler_params=params,
    )(pivots[0], summed[0], col[None])
    return inner_inverse, lower_factor, own[None]


def solution(mesh):
    placed = (
        P(("rows", "cols"), None, None),
        P("rows", "cols", None, None),
        P("rows", "cols", None, None),
        P("rows", "cols", None),
        P("rows", "cols"),
        P("rows"),
    )
    return jax.shard_map(
        shards,
        mesh=mesh,
        in_specs=placed,
        out_specs=(
            P(("rows", "cols"), None, None),
            P("rows", "cols", None, None),
            P("rows", "cols", None),
        ),
        check_vma=False,
    )
```

```python
import functools

import jax
import jax.numpy as jnp
from jax import lax
from jax.experimental import pallas as pl
from jax.experimental.pallas import tpu as pltpu
from jax.sharding import PartitionSpec as P

HIGH = lax.Precision.HIGH
VMEM = pl.BlockSpec(memory_space=pltpu.VMEM)
SMEM = pl.BlockSpec(memory_space=pltpu.SMEM)
GRANT = 48 << 20
CORES, RING, DEPTH, TILE = 2, 4, 8, 8


def dot(a, b):
    return lax.dot_general(a, b, (((1,), (0,)), ((), ())), precision=HIGH, preferred_element_type=jnp.float32)


def eliminate(slabs, first, ahead):
    depth, width = slabs[0].shape
    lanes = lax.broadcasted_iota(jnp.int32, (1, width), 1)
    rows = lax.broadcasted_iota(jnp.int32, (depth, width), 0)
    for start in range(0, depth, ahead):
        base = first + start
        spread = [
            [jnp.broadcast_to(slab[:, base + t : base + t + 1], (depth, width)) for t in range(ahead)]
            for slab in slabs
        ]
        for t in range(ahead):
            k = start + t
            at_lane = (lanes == base + t).astype(jnp.float32)
            at_row = (rows == k).astype(jnp.float32)
            for index, slab in enumerate(slabs):
                columns = spread[index]
                inverse = 1.0 / columns[t][k : k + 1, :]
                pivot_row = (slab[k : k + 1, :] + at_lane) * inverse
                column = columns[t] - at_row
                for u in range(t + 1, ahead):
                    columns[u] = columns[u] - column * (columns[u][k : k + 1, :] * inverse)
                slabs[index] = slab - column * pivot_row
    return slabs


def invert(ref, members, panel, ahead):
    size = ref.shape[-1]
    lanes = lax.broadcasted_iota(jnp.int32, (1, size), 1)
    for first in range(0, size, panel):
        slabs = eliminate([ref[b, first : first + panel, :] for b in members], first, ahead)
        inside = (lanes >= first) & (lanes < first + panel)
        for b, slab in zip(members, slabs):
            whole = ref[b]
            update = dot(whole[:, first : first + panel], slab)
            ref[b] = jnp.where(inside, 0.0, whole) - update
            ref[b, first : first + panel, :] = slab


def interiors_kernel(pivots, out):
    out[...] = pivots[...]
    invert(out, range(pivots.shape[0]), 8, 8)


def couplings_kernel(group, first_slot, ids, counts, inverses, lower, upper, factor, schur):
    step = pl.program_id(0)

    @pl.when(step == 0)
    def _():
        schur[...] = jnp.zeros_like(schur)

    products = []
    for g in range(group):
        live = first_slot[0] < counts[step * group + g]
        value = jnp.where(live, dot(lower[g, 0], inverses[g]), 0.0)
        factor[g, 0] = value
        products.append(dot(value, upper[g, 0]))
    for g in range(group):
        j = ids[step * group + g]
        core, spot = lax.rem(j, CORES), lax.div(j, CORES)
        for quarter in range(RING):
            for half in range(2):
                for way in range(2):
                    row = quarter * 32 + half * 16 + way * TILE
                    at = (core, half, way, quarter, spot)
                    schur[at] = schur[at] + products[g][row : row + TILE, :]


class Ring:
    def __init__(self, axis, step, me, blocks, own, land, send, recv):
        self.blocks, self.own, self.land, self.send, self.recv = blocks, own, land, send, recv
        self.me, self.axis, self.step = me, axis, step
        self.sent = []

    def at(self, offset):
        return lax.rem(self.me + offset, RING)

    def copy(self, slot, source, offset):
        copy = pltpu.make_async_remote_copy(
            src_ref=source,
            dst_ref=self.land.at[slot],
            send_sem=self.send.at[slot],
            recv_sem=self.recv.at[slot],
            device_id=self.step(self.at(offset)),
            device_id_type=pl.DeviceIdType.MESH,
        )
        copy.start()
        self.sent.append(copy)
        return copy

    def first(self):
        self.relay_up = self.copy(0, self.blocks(1, self.at(2)), 1)
        self.relay_down = self.copy(1, self.blocks(0, self.at(2)), 3)
        self.last_up = self.copy(2, self.blocks(0, self.at(1)), 1)
        self.last_down = self.copy(3, self.blocks(1, self.at(3)), 3)

    def second(self):
        self.relay_up.wait_recv()
        block = self.blocks(1, self.at(1))
        block[...] = block[...] + self.land[0]
        self.sum_up = self.copy(4, block, 1)
        self.relay_down.wait_recv()
        block = self.blocks(0, self.at(3))
        block[...] = block[...] + self.land[1]
        self.sum_down = self.copy(5, block, 3)

    def third(self):
        self.last_up.wait_recv()
        self.sum_down.wait_recv()
        self.own(0, self.blocks(0, self.me)[...] + (self.land[2] + self.land[5]))
        self.last_down.wait_recv()
        self.sum_up.wait_recv()
        self.own(1, self.blocks(1, self.me)[...] + (self.land[3] + self.land[4]))

    def drain(self):
        for copy in self.sent:
            copy.wait_send()


def separators_kernel(
    schur, pivots, out, mine, other, x_wide, y_wide, x_part, y_part, x_thin, y_thin, stack, column, work, whole,
    send, recv, load, core_send, core_recv, z_send, z_recv, q_send, q_recv,
):
    row, x = lax.axis_index("rows"), lax.axis_index("cols")
    core = lax.rem(row, CORES)
    z = lax.rem(lax.div(row, CORES), DEPTH)
    y = lax.div(row, CORES * DEPTH)

    def device(x_at, y_at, z_at, core_at):
        return {"rows": (y_at * DEPTH + z_at) * CORES + core_at, "cols": x_at}

    sibling = device(x, y, z, 1 - core)
    along_x = lambda at: device(at, y, z, core)
    along_y = lambda at: device(x, at, z, core)
    along_z = lambda at: device(x, y, at, core)

    barrier = pltpu.get_barrier_semaphore()
    greeted = [sibling]
    greeted += [along_x(lax.rem(x + t, RING)) for t in (1, 2, 3)]
    greeted += [along_y(lax.rem(y + t, RING)) for t in (1, 3)]
    greeted += [along_z(lax.rem(z + t, DEPTH)) for t in range(1, DEPTH)]
    for peer in greeted:
        pl.semaphore_signal(barrier, inc=1, device_id=peer, device_id_type=pl.DeviceIdType.MESH)

    loads = []
    for part in range(4):
        half, way = part // 2, part % 2
        copy = pltpu.make_async_copy(schur.at[core, half, way], mine.at[half, way], load.at[part])
        copy.start()
        loads.append(copy)
    pl.semaphore_wait(barrier, len(greeted))

    crossed = []
    for part in range(4):
        half, way = part // 2, part % 2
        copy = pltpu.make_async_remote_copy(
            src_ref=schur.at[1 - core, half, way],
            dst_ref=other.at[half, way],
            send_sem=core_send.at[part],
            recv_sem=core_recv.at[part],
            device_id=sibling,
            device_id_type=pl.DeviceIdType.MESH,
        )
        copy.start()
        crossed.append(copy)
    for part in range(4):
        half, way = part // 2, part % 2
        loads[part].wait()
        crossed[part].wait_recv()
        mine[half, way] = mine[half, way] + other[half, way]

    def keep_x(way, value):
        x_part[way] = value

    def keep_y(way, value):
        y_part[way] = value

    wide_x = Ring("x", along_x, x, lambda way, d: mine.at[0, way, d], keep_x, x_wide, send.at[0], recv.at[0])
    wide_y = Ring(
        "y", along_y, y, lambda way, d: mine.at[1, way, :, pl.ds(d * DEPTH, DEPTH)], keep_y, y_wide,
        send.at[1], recv.at[1],
    )
    for stage in ("first", "second", "third"):
        getattr(wide_x, stage)()
        getattr(wide_y, stage)()

    def stack_x(way, value):
        for t in range(DEPTH):
            stack[t, way] = value[t]

    def stack_y(way, value):
        for t in range(DEPTH):
            stack[t, 2 + way] = value[t]

    thin_y = Ring(
        "y", along_y, y, lambda way, d: x_part.at[way, pl.ds(d * DEPTH, DEPTH)], stack_x, y_thin,
        send.at[2], recv.at[2],
    )
    thin_x = Ring("x", along_x, x, lambda way, d: y_part.at[way, d], stack_y, x_thin, send.at[3], recv.at[3])
    for stage in ("first", "second", "third"):
        getattr(thin_y, stage)()
        getattr(thin_x, stage)()

    spread = []
    for t in range(1, DEPTH):
        to = lax.rem(z + t, DEPTH)
        copy = pltpu.make_async_remote_copy(
            src_ref=stack.at[to],
            dst_ref=column.at[t - 1],
            send_sem=z_send.at[t - 1],
            recv_sem=z_recv.at[t - 1],
            device_id=along_z(to),
            device_id_type=pl.DeviceIdType.MESH,
        )
        copy.start()
        spread.append(copy)
    total = stack[z]
    for t in range(1, DEPTH):
        spread[t - 1].wait_recv()
        total = total + column[t - 1]

    rows = pivots.shape[0]
    work[x] = pivots[...] - total.reshape(rows, total.shape[-1])
    quarters = []
    for t in range(1, RING):
        copy = pltpu.make_async_remote_copy(
            src_ref=work.at[x],
            dst_ref=work.at[x],
            send_sem=q_send.at[t - 1],
            recv_sem=q_recv.at[t - 1],
            device_id=along_x(lax.rem(x + t, RING)),
            device_id_type=pl.DeviceIdType.MESH,
        )
        copy.start()
        quarters.append(copy)
    for copy in quarters:
        copy.wait()
    for ring in (wide_x, wide_y, thin_x, thin_y):
        ring.drain()
    for copy in crossed + spread:
        copy.wait_send()

    whole[0] = work[...].reshape(whole.shape[1:])
    invert(whole, range(1), 32, 16)
    out[...] = whole[0, pl.ds(pl.multiple_of(x * rows, rows), rows), :]


def shards(inner_pivots, lower_blocks, upper_blocks, separator_pivots, separator_ids, coupling_count):
    f32 = jnp.float32
    count, size = inner_pivots.shape[0], inner_pivots.shape[1]
    couplings = lower_blocks.shape[0]
    col = lax.axis_index("cols").astype(jnp.int32)
    separators = separator_pivots.shape[0] * lax.axis_size("rows")
    params = pltpu.CompilerParams(vmem_limit_bytes=GRANT)

    inner_inverse = pl.pallas_call(
        interiors_kernel,
        out_shape=jax.ShapeDtypeStruct((count, size, size), f32),
        in_specs=[VMEM],
        out_specs=VMEM,
        compiler_params=params,
    )(inner_pivots)
    inverses = lax.all_gather(inner_inverse, "cols", axis=0, tiled=True)

    group = 6
    spots = separators // CORES
    schur_shape = (CORES, 2, 2, RING, spots, TILE, size)
    block = pl.BlockSpec((group, 1, size, size), lambda s, *_: (s, 0, 0, 0))
    lower_factor, schur = pl.pallas_call(
        functools.partial(couplings_kernel, group),
        grid_spec=pltpu.PrefetchScalarGridSpec(
            num_scalar_prefetch=3,
            grid=(couplings // group,),
            in_specs=[pl.BlockSpec((group, size, size), lambda s, *_: (s, 0, 0)), block, block],
            out_specs=[block, pl.BlockSpec(schur_shape, lambda s, *_: (0,) * len(schur_shape))],
        ),
        out_shape=[
            jax.ShapeDtypeStruct(lower_blocks.shape, f32),
            jax.ShapeDtypeStruct(schur_shape, f32),
        ],
        compiler_params=params,
    )(col[None], separator_ids.reshape(-1), coupling_count, inverses, lower_blocks, upper_blocks)

    rows = separator_pivots.shape[1]
    tile = (TILE, size)
    own = pl.pallas_call(
        separators_kernel,
        out_shape=jax.ShapeDtypeStruct((rows, size), f32),
        in_specs=[pl.BlockSpec(memory_space=pl.ANY), VMEM],
        out_specs=VMEM,
        scratch_shapes=[
            pltpu.VMEM(schur_shape[1:], f32),
            pltpu.VMEM(schur_shape[1:], f32),
            pltpu.VMEM((6, spots) + tile, f32),
            pltpu.VMEM((6, RING, DEPTH) + tile, f32),
            pltpu.VMEM((2, spots) + tile, f32),
            pltpu.VMEM((2, RING, DEPTH) + tile, f32),
            pltpu.VMEM((6, DEPTH) + tile, f32),
            pltpu.VMEM((6, DEPTH) + tile, f32),
            pltpu.VMEM((DEPTH, 4) + tile, f32),
            pltpu.VMEM((DEPTH - 1, 4) + tile, f32),
            pltpu.VMEM((RING, rows, size), f32),
            pltpu.VMEM((1, size, size), f32),
            pltpu.SemaphoreType.DMA((4, 6)),
            pltpu.SemaphoreType.DMA((4, 6)),
            pltpu.SemaphoreType.DMA((4,)),
            pltpu.SemaphoreType.DMA((4,)),
            pltpu.SemaphoreType.DMA((4,)),
            pltpu.SemaphoreType.DMA((DEPTH - 1,)),
            pltpu.SemaphoreType.DMA((DEPTH - 1,)),
            pltpu.SemaphoreType.DMA((RING - 1,)),
            pltpu.SemaphoreType.DMA((RING - 1,)),
        ],
        compiler_params=pltpu.CompilerParams(vmem_limit_bytes=GRANT, collective_id=1, has_side_effects=True),
    )(schur, separator_pivots[0])
    return inner_inverse, lower_factor, own[None]


def solution(mesh):
    placed = (
        P(("rows", "cols"), None, None),
        P("rows", "cols", None, None),
        P("rows", "cols", None, None),
        P("rows", "cols", None),
        P("rows", "cols"),
        P("rows"),
    )
    return jax.shard_map(
        shards,
        mesh=mesh,
        in_specs=placed,
        out_specs=(
            P(("rows", "cols"), None, None),
            P("rows", "cols", None, None),
            P("rows", "cols", None),
        ),
        check_vma=False,
    )
```

```python
import functools

import jax
import jax.numpy as jnp
from jax import lax
from jax.experimental import pallas as pl
from jax.experimental.pallas import tpu as pltpu
from jax.sharding import PartitionSpec as P

HIGH = lax.Precision.HIGH
VMEM = pl.BlockSpec(memory_space=pltpu.VMEM)
SMEM = pl.BlockSpec(memory_space=pltpu.SMEM)
ANY = pl.BlockSpec(memory_space=pl.ANY)
GRANT = 48 << 20
CORES, RING, DEPTH, TILE, GROUPS = 2, 4, 8, 8, 2


def dot(a, b):
    return lax.dot_general(a, b, (((1,), (0,)), ((), ())), precision=HIGH, preferred_element_type=jnp.float32)


def eliminate(slabs, first, ahead):
    depth, width = slabs[0].shape
    lanes = lax.broadcasted_iota(jnp.int32, (1, width), 1)
    rows = lax.broadcasted_iota(jnp.int32, (depth, width), 0)
    for start in range(0, depth, ahead):
        base = first + start
        spread = [
            [jnp.broadcast_to(slab[:, base + t : base + t + 1], (depth, width)) for t in range(ahead)]
            for slab in slabs
        ]
        for t in range(ahead):
            k = start + t
            at_lane = (lanes == base + t).astype(jnp.float32)
            at_row = (rows == k).astype(jnp.float32)
            for index, slab in enumerate(slabs):
                columns = spread[index]
                inverse = 1.0 / columns[t][k : k + 1, :]
                pivot_row = (slab[k : k + 1, :] + at_lane) * inverse
                column = columns[t] - at_row
                for u in range(t + 1, ahead):
                    columns[u] = columns[u] - column * (columns[u][k : k + 1, :] * inverse)
                slabs[index] = slab - column * pivot_row
    return slabs


def eliminate_by_tile(slabs, first):
    depth, width = slabs[0].shape
    lanes = lax.broadcasted_iota(jnp.int32, (1, width), 1)
    rows = lax.broadcasted_iota(jnp.int32, (TILE, width), 0)
    tiles = [[slab[t : t + TILE, :] for t in range(0, depth, TILE)] for slab in slabs]
    for q in range(depth // TILE):
        base = first + q * TILE
        inside = (lanes >= base) & (lanes < base + TILE)
        for parts in tiles:
            spread = [
                [jnp.broadcast_to(part[:, base + t : base + t + 1], (TILE, width)) for t in range(TILE)]
                for part in parts
            ]
            pivot, columns = parts[q], spread[q]
            for t in range(TILE):
                at_lane = (lanes == base + t).astype(jnp.float32)
                at_row = (rows == t).astype(jnp.float32)
                inverse = 1.0 / columns[t][t : t + 1, :]
                pivot_row = (pivot[t : t + 1, :] + at_lane) * inverse
                column = columns[t] - at_row
                for u in range(t + 1, TILE):
                    columns[u] = columns[u] - column * (columns[u][t : t + 1, :] * inverse)
                pivot = pivot - column * pivot_row
            parts[q] = pivot
            for other in range(len(parts)):
                if other != q:
                    value = jnp.where(inside, 0.0, parts[other])
                    for t in range(TILE):
                        value = value - spread[other][t] * pivot[t : t + 1, :]
                    parts[other] = value
    return [jnp.concatenate(parts, axis=0) for parts in tiles]


def invert(refs, panel, eliminate_slabs):
    size = refs[0].shape[-1]
    lanes = lax.broadcasted_iota(jnp.int32, (1, size), 1)
    for first in range(0, size, panel):
        slabs = eliminate_slabs([ref[first : first + panel, :] for ref in refs], first)
        inside = (lanes >= first) & (lanes < first + panel)
        for ref, slab in zip(refs, slabs):
            whole = ref[...]
            update = dot(whole[:, first : first + panel], slab)
            ref[...] = jnp.where(inside, 0.0, whole) - update
            ref[first : first + panel, :] = slab


class Ring:
    def __init__(self, axis, step, me, blocks, own, land, send, recv):
        self.blocks, self.own, self.land, self.send, self.recv = blocks, own, land, send, recv
        self.me, self.axis, self.step = me, axis, step
        self.sent = []

    def at(self, offset):
        return lax.rem(self.me + offset, RING)

    def copy(self, slot, source, offset):
        copy = pltpu.make_async_remote_copy(
            src_ref=source,
            dst_ref=self.land.at[slot],
            send_sem=self.send.at[slot],
            recv_sem=self.recv.at[slot],
            device_id=self.step(self.at(offset)),
            device_id_type=pl.DeviceIdType.MESH,
        )
        copy.start()
        self.sent.append(copy)
        return copy

    def first(self):
        self.relay_up = self.copy(0, self.blocks(1, self.at(2)), 1)
        self.relay_down = self.copy(1, self.blocks(0, self.at(2)), 3)
        self.last_up = self.copy(2, self.blocks(0, self.at(1)), 1)
        self.last_down = self.copy(3, self.blocks(1, self.at(3)), 3)

    def second(self):
        self.relay_up.wait_recv()
        block = self.blocks(1, self.at(1))
        block[...] = block[...] + self.land[0]
        self.sum_up = self.copy(4, block, 1)
        self.relay_down.wait_recv()
        block = self.blocks(0, self.at(3))
        block[...] = block[...] + self.land[1]
        self.sum_down = self.copy(5, block, 3)

    def third(self):
        self.last_up.wait_recv()
        self.sum_down.wait_recv()
        self.own(0, self.blocks(0, self.me)[...] + (self.land[2] + self.land[5]))
        self.last_down.wait_recv()
        self.sum_up.wait_recv()
        self.own(1, self.blocks(1, self.me)[...] + (self.land[3] + self.land[4]))

    def drain(self):
        for copy in self.sent:
            copy.wait_send()


def kernel(
    ids, ids_row, counts, pivots, lower, upper, own_pivots, inner, factor, out,
    inverses, low, up, fac, chain, link, theirs, mine, other, x_wide, y_wide, x_part, y_part, x_thin, y_thin,
    stack, column, work, whole,
    pivot_load, block_load, gather_send, gather_recv, inner_store, factor_store,
    send, recv, core_send, core_recv, z_send, z_recv, q_send, q_recv,
):
    row, x = lax.axis_index("rows"), lax.axis_index("cols")
    core = lax.rem(row, CORES)
    z = lax.rem(lax.div(row, CORES), DEPTH)
    y = lax.div(row, CORES * DEPTH)
    count, size = pivots.shape[0], pivots.shape[-1]
    couplings, separators = counts.shape[0], 2 * theirs.shape[3]
    group = count // GROUPS
    part = group // 2

    def device(x_at, y_at, z_at, core_at):
        return {"rows": (y_at * DEPTH + z_at) * CORES + core_at, "cols": x_at}

    sibling = device(x, y, z, 1 - core)
    along_x = lambda at: device(at, y, z, core)
    along_y = lambda at: device(x, at, z, core)
    along_z = lambda at: device(x, y, at, core)

    barrier = pltpu.get_barrier_semaphore()
    greeted = [sibling]
    greeted += [along_x(lax.rem(x + t, RING)) for t in (1, 2, 3)]
    greeted += [along_y(lax.rem(y + t, RING)) for t in (1, 3)]
    greeted += [along_z(lax.rem(z + t, DEPTH)) for t in range(1, DEPTH)]
    for peer in greeted:
        pl.semaphore_signal(barrier, inc=1, device_id=peer, device_id_type=pl.DeviceIdType.MESH)

    def source(offset):
        return lax.rem(x + offset, RING)

    def load_pivots(g):
        members = pl.ds(g * group, group)
        return pltpu.make_async_copy(pivots.at[members], inverses.at[x, members], pivot_load.at[g])

    def load_blocks(offset):
        members = pl.ds(source(offset) * count, count)
        return (
            pltpu.make_async_copy(lower.at[members, 0], low.at[members], block_load.at[0, offset]),
            pltpu.make_async_copy(upper.at[members, 0], up.at[members], block_load.at[1, offset]),
        )

    for g in range(GROUPS):
        load_pivots(g).start()
    for offset in range(RING):
        for copy in load_blocks(offset):
            copy.start()
    pl.semaphore_wait(barrier, len(greeted))

    def gather(kind, g):
        block = inverses.at[x, pl.ds(g * group, group)]
        if kind == 2:
            block = inverses.at[source(3), pl.ds(g * group, part)]
        if kind == 3:
            block = inverses.at[source(1), pl.ds(g * group + part, part)]
        return pltpu.make_async_remote_copy(
            src_ref=block,
            dst_ref=block,
            send_sem=gather_send.at[kind, g],
            recv_sem=gather_recv.at[kind, g],
            device_id=along_x(source(1 if kind % 2 == 0 else 3)),
            device_id_type=pl.DeviceIdType.MESH,
        )

    def make_inverses(g, carry):
        load_pivots(g).wait()
        invert([inverses.at[x, g * group + b] for b in range(group)], 16, eliminate_by_tile)
        gather(0, g).start()
        gather(1, g).start()
        return carry

    lax.fori_loop(0, GROUPS, make_inverses, 0)
    store_inner = pltpu.make_async_copy(inverses.at[x], inner, inner_store)
    store_inner.start()

    lane = lax.broadcasted_iota(jnp.int32, (1, couplings), 1)
    owner, local = lax.div(lane, count), lax.rem(lane, count)
    behind = lax.rem(owner + RING - x, RING)
    turn = jnp.where(behind == 3, 0, jnp.where(behind == 1, group, 2 * group))
    later = count + lax.div(local, group) * 3 * group + turn + lax.rem(local, group)
    place = jnp.where(behind == 0, local, later)
    named = ids_row[...]

    def newest(target, limit):
        found = jnp.max(jnp.where((named == target) & (place < limit), place, -1))
        return jnp.where(found < 0, couplings, found)

    def interior(n):
        late = n - count
        third = lax.div(lax.rem(late, 3 * group), group)
        offset = jnp.where(third == 0, 3, jnp.where(third == 1, 1, 2))
        in_own = lax.div(late, 3 * group) * group + lax.rem(late, group)
        return jnp.where(n < count, x * count + n, source(offset) * count + in_own)

    def find_previous(n, carry):
        link[n] = newest(ids[interior(n)], n)
        return carry

    def find_last(j, carry):
        link[couplings + j] = newest(j, couplings)
        return carry

    lax.fori_loop(0, couplings, find_previous, 0, unroll=8)
    lax.fori_loop(0, separators, find_last, 0, unroll=8)
    chain[couplings] = jnp.zeros((size, size), jnp.float32)

    stores = []

    def couple(offset, first, length, place_first):
        base = source(offset) * count + first
        for b in range(length):
            i, n = base + b, place_first + b
            value = jnp.where(x < counts[i], dot(low[i], inverses[source(offset), first + b]), 0.0)
            fac[i] = value
            chain[n] = dot(value, up[i]) + chain[link[n]]
        members = pl.ds(base, length)
        copy = pltpu.make_async_copy(fac.at[members], factor.at[members, 0], factor_store.at[len(stores)])
        copy.start()
        stores.append(copy)

    def await_blocks(offset):
        for copy in load_blocks(offset):
            copy.wait()

    await_blocks(0)
    gather(0, 0).wait_recv()
    gather(2, 0).start()
    gather(1, 0).wait_recv()
    gather(3, 0).start()
    for g in range(GROUPS):
        couple(0, g * group, group, g * group)
    for offset in (3, 1, 2):
        await_blocks(offset)
    for g in range(GROUPS):
        place_first = count + g * 3 * group
        if g > 0:
            gather(0, g).wait_recv()
            gather(2, g).start()
            gather(1, g).wait_recv()
            gather(3, g).start()
        couple(3, g * group, group, place_first)
        couple(1, g * group, group, place_first + group)
        gather(2, g).wait_recv()
        couple(2, g * group, part, place_first + 2 * group)
        gather(3, g).wait_recv()
        couple(2, g * group + part, part, place_first + 2 * group + part)

    def lay_out(parity, into):
        def body(spot, carry):
            value = chain[link[couplings + spot * CORES + parity]]
            for quarter in range(RING):
                for half in range(2):
                    for way in range(2):
                        at = quarter * 32 + half * 16 + way * TILE
                        into[half, way, quarter, spot] = value[at : at + TILE, :]
            return carry

        lax.fori_loop(0, separators // CORES, body, 0, unroll=4)

    lay_out(1 - core, theirs)

    crossed = []
    for piece in range(4):
        half, way = piece // 2, piece % 2
        copy = pltpu.make_async_remote_copy(
            src_ref=theirs.at[half, way],
            dst_ref=other.at[half, way],
            send_sem=core_send.at[piece],
            recv_sem=core_recv.at[piece],
            device_id=sibling,
            device_id_type=pl.DeviceIdType.MESH,
        )
        copy.start()
        crossed.append(copy)
    lay_out(core, mine)
    for piece in range(4):
        half, way = piece // 2, piece % 2
        crossed[piece].wait_recv()
        mine[half, way] = mine[half, way] + other[half, way]

    def keep_x(way, value):
        x_part[way] = value

    def keep_y(way, value):
        y_part[way] = value

    wide_x = Ring("x", along_x, x, lambda way, d: mine.at[0, way, d], keep_x, x_wide, send.at[0], recv.at[0])
    wide_y = Ring(
        "y", along_y, y, lambda way, d: mine.at[1, way, :, pl.ds(d * DEPTH, DEPTH)], keep_y, y_wide,
        send.at[1], recv.at[1],
    )
    for stage in ("first", "second", "third"):
        getattr(wide_x, stage)()
        getattr(wide_y, stage)()

    def stack_x(way, value):
        for t in range(DEPTH):
            stack[t, way] = value[t]

    def stack_y(way, value):
        for t in range(DEPTH):
            stack[t, 2 + way] = value[t]

    thin_y = Ring(
        "y", along_y, y, lambda way, d: x_part.at[way, pl.ds(d * DEPTH, DEPTH)], stack_x, y_thin,
        send.at[2], recv.at[2],
    )
    thin_x = Ring("x", along_x, x, lambda way, d: y_part.at[way, d], stack_y, x_thin, send.at[3], recv.at[3])
    for stage in ("first", "second", "third"):
        getattr(thin_y, stage)()
        getattr(thin_x, stage)()

    spread = []
    for t in range(1, DEPTH):
        to = lax.rem(z + t, DEPTH)
        copy = pltpu.make_async_remote_copy(
            src_ref=stack.at[to],
            dst_ref=column.at[t - 1],
            send_sem=z_send.at[t - 1],
            recv_sem=z_recv.at[t - 1],
            device_id=along_z(to),
            device_id_type=pl.DeviceIdType.MESH,
        )
        copy.start()
        spread.append(copy)
    total = stack[z]
    for t in range(1, DEPTH):
        spread[t - 1].wait_recv()
        total = total + column[t - 1]

    rows = own_pivots.shape[0]
    work[x] = own_pivots[...] - total.reshape(rows, total.shape[-1])
    quarters = []
    for t in range(1, RING):
        copy = pltpu.make_async_remote_copy(
            src_ref=work.at[x],
            dst_ref=work.at[x],
            send_sem=q_send.at[t - 1],
            recv_sem=q_recv.at[t - 1],
            device_id=along_x(lax.rem(x + t, RING)),
            device_id_type=pl.DeviceIdType.MESH,
        )
        copy.start()
        quarters.append(copy)
    for copy in quarters:
        copy.wait()
    for ring in (wide_x, wide_y, thin_x, thin_y):
        ring.drain()
    for copy in crossed + spread:
        copy.wait_send()

    whole[...] = work[...].reshape(whole.shape)
    invert([whole], 32, functools.partial(eliminate, ahead=16))
    out[...] = whole[pl.ds(pl.multiple_of(x * rows, rows), rows), :]
    for g in range(GROUPS):
        for kind in range(4):
            gather(kind, g).wait_send()
    for copy in stores + [store_inner]:
        copy.wait()


def shards(inner_pivots, lower_blocks, upper_blocks, separator_pivots, separator_ids, coupling_count):
    f32 = jnp.float32
    count, size = inner_pivots.shape[0], inner_pivots.shape[1]
    couplings = lower_blocks.shape[0]
    separators = separator_pivots.shape[0] * lax.axis_size("rows")
    rows = separator_pivots.shape[1]
    spots = separators // CORES
    tile = (TILE, size)
    block = (size, size)
    dma = pltpu.SemaphoreType.DMA
    vmem = lambda *shape: pltpu.VMEM(shape, f32)
    inner_inverse, lower_factor, own = pl.pallas_call(
        kernel,
        out_shape=[
            jax.ShapeDtypeStruct(inner_pivots.shape, f32),
            jax.ShapeDtypeStruct(lower_blocks.shape, f32),
            jax.ShapeDtypeStruct((rows, size), f32),
        ],
        in_specs=[SMEM, VMEM, SMEM, ANY, ANY, ANY, VMEM],
        out_specs=[ANY, ANY, VMEM],
        scratch_shapes=[
            vmem(RING, count, *block),
            vmem(couplings, *block),
            vmem(couplings, *block),
            vmem(couplings, *block),
            vmem(couplings + 1, *block),
            pltpu.SMEM((couplings + separators,), jnp.int32),
            vmem(2, 2, RING, spots, *tile),
            vmem(2, 2, RING, spots, *tile),
            vmem(2, 2, RING, spots, *tile),
            vmem(6, spots, *tile),
            vmem(6, RING, DEPTH, *tile),
            vmem(2, spots, *tile),
            vmem(2, RING, DEPTH, *tile),
            vmem(6, DEPTH, *tile),
            vmem(6, DEPTH, *tile),
            vmem(DEPTH, 4, *tile),
            vmem(DEPTH - 1, 4, *tile),
            vmem(RING, rows, size),
            vmem(*block),
            dma((GROUPS,)),
            dma((2, RING)),
            dma((4, GROUPS)),
            dma((4, GROUPS)),
            dma,
            dma((5 * GROUPS,)),
            dma((4, 6)),
            dma((4, 6)),
            dma((4,)),
            dma((4,)),
            dma((DEPTH - 1,)),
            dma((DEPTH - 1,)),
            dma((RING - 1,)),
            dma((RING - 1,)),
        ],
        compiler_params=pltpu.CompilerParams(vmem_limit_bytes=GRANT, collective_id=0, has_side_effects=True),
    )(
        separator_ids.reshape(-1),
        separator_ids.reshape(1, -1),
        coupling_count,
        inner_pivots,
        lower_blocks,
        upper_blocks,
        separator_pivots[0],
    )
    return inner_inverse, lower_factor, own[None]


def solution(mesh):
    placed = (
        P(("rows", "cols"), None, None),
        P("rows", "cols", None, None),
        P("rows", "cols", None, None),
        P("rows", "cols", None),
        P("rows", "cols"),
        P("rows"),
    )
    return jax.shard_map(
        shards,
        mesh=mesh,
        in_specs=placed,
        out_specs=(
            P(("rows", "cols"), None, None),
            P("rows", "cols", None, None),
            P("rows", "cols", None),
        ),
        check_vma=False,
    )
```

```python
import functools

import jax
import jax.numpy as jnp
from jax import lax
from jax.experimental import pallas as pl
from jax.experimental.pallas import tpu as pltpu
from jax.sharding import PartitionSpec as P

HIGH = lax.Precision.HIGH
VMEM = pl.BlockSpec(memory_space=pltpu.VMEM)
HBM = pl.BlockSpec(memory_space=pltpu.HBM)
ANY = pl.BlockSpec(memory_space=pl.ANY)
GRANT = 63 << 20
CORES, RING, DEPTH, TILE = 2, 4, 8, 8


def dot(a, b):
    return lax.dot_general(a, b, (((1,), (0,)), ((), ())), precision=HIGH, preferred_element_type=jnp.float32)


def eliminate(slabs, first, ahead):
    depth, width = slabs[0].shape
    lanes = lax.broadcasted_iota(jnp.int32, (1, width), 1)
    rows = lax.broadcasted_iota(jnp.int32, (depth, width), 0)
    for start in range(0, depth, ahead):
        base = first + start
        spread = [
            [jnp.broadcast_to(slab[:, base + t : base + t + 1], (depth, width)) for t in range(ahead)]
            for slab in slabs
        ]
        for t in range(ahead):
            k = start + t
            at_lane = (lanes == base + t).astype(jnp.float32)
            at_row = (rows == k).astype(jnp.float32)
            for index, slab in enumerate(slabs):
                columns = spread[index]
                inverse = 1.0 / columns[t][k : k + 1, :]
                pivot_row = (slab[k : k + 1, :] + at_lane) * inverse
                column = columns[t] - at_row
                for u in range(t + 1, ahead):
                    columns[u] = columns[u] - column * (columns[u][k : k + 1, :] * inverse)
                slabs[index] = slab - column * pivot_row
    return slabs


def eliminate_by_tile(slabs, first):
    depth, width = slabs[0].shape
    lanes = lax.broadcasted_iota(jnp.int32, (1, width), 1)
    rows = lax.broadcasted_iota(jnp.int32, (TILE, width), 0)
    tiles = [[slab[t : t + TILE, :] for t in range(0, depth, TILE)] for slab in slabs]
    for q in range(depth // TILE):
        base = first + q * TILE
        inside = (lanes >= base) & (lanes < base + TILE)
        for parts in tiles:
            spread = [
                [jnp.broadcast_to(part[:, base + t : base + t + 1], (TILE, width)) for t in range(TILE)]
                for part in parts
            ]
            pivot, columns = parts[q], spread[q]
            for t in range(TILE):
                at_lane = (lanes == base + t).astype(jnp.float32)
                at_row = (rows == t).astype(jnp.float32)
                inverse = 1.0 / columns[t][t : t + 1, :]
                pivot_row = (pivot[t : t + 1, :] + at_lane) * inverse
                column = columns[t] - at_row
                for u in range(t + 1, TILE):
                    columns[u] = columns[u] - column * (columns[u][t : t + 1, :] * inverse)
                pivot = pivot - column * pivot_row
            parts[q] = pivot
            for other in range(len(parts)):
                if other != q:
                    value = jnp.where(inside, 0.0, parts[other])
                    for t in range(TILE):
                        value = value - spread[other][t] * pivot[t : t + 1, :]
                    parts[other] = value
    return [jnp.concatenate(parts, axis=0) for parts in tiles]


def invert(refs, panel, eliminate_slabs, after_first=None):
    size = refs[0].shape[-1]
    lanes = lax.broadcasted_iota(jnp.int32, (1, size), 1)
    for first in range(0, size, panel):
        slabs = eliminate_slabs([ref[first : first + panel, :] for ref in refs], first)
        inside = (lanes >= first) & (lanes < first + panel)
        for ref, slab in zip(refs, slabs):
            whole = ref[...]
            update = dot(whole[:, first : first + panel], slab)
            ref[...] = jnp.where(inside, 0.0, whole) - update
            ref[first : first + panel, :] = slab
        if first == 0 and after_first is not None:
            after_first()


class Ring:
    def __init__(self, axis, step, me, blocks, own, land, send, recv):
        self.blocks, self.own, self.land, self.send, self.recv = blocks, own, land, send, recv
        self.me, self.axis, self.step = me, axis, step
        self.sent = []

    def at(self, offset):
        return lax.rem(self.me + offset, RING)

    def copy(self, slot, source, offset):
        copy = pltpu.make_async_remote_copy(
            src_ref=source,
            dst_ref=self.land.at[slot],
            send_sem=self.send.at[slot],
            recv_sem=self.recv.at[slot],
            device_id=self.step(self.at(offset)),
            device_id_type=pl.DeviceIdType.MESH,
        )
        copy.start()
        self.sent.append(copy)
        return copy

    def first(self):
        self.relay_up = self.copy(0, self.blocks(1, self.at(2)), 1)
        self.relay_down = self.copy(1, self.blocks(0, self.at(2)), 3)
        self.last_up = self.copy(2, self.blocks(0, self.at(1)), 1)
        self.last_down = self.copy(3, self.blocks(1, self.at(3)), 3)

    def second(self):
        self.relay_up.wait_recv()
        block = self.blocks(1, self.at(1))
        block[...] = block[...] + self.land[0]
        self.sum_up = self.copy(4, block, 1)
        self.relay_down.wait_recv()
        block = self.blocks(0, self.at(3))
        block[...] = block[...] + self.land[1]
        self.sum_down = self.copy(5, block, 3)

    def third(self):
        self.last_up.wait_recv()
        self.sum_down.wait_recv()
        self.own(0, self.blocks(0, self.me)[...] + (self.land[2] + self.land[5]))
        self.last_down.wait_recv()
        self.sum_up.wait_recv()
        self.own(1, self.blocks(1, self.me)[...] + (self.land[3] + self.land[4]))

    def drain(self):
        for copy in self.sent:
            copy.wait_send()


RAW = 2
PARTS = 4
PIECES = ((0, RAW), (RAW, 6), (RAW + 6, 4))
BLOCKS = (
    (0, 0, 12), (3, 0, 2), (1, 0, 2), (2, 0, 2), (3, 2, 6), (1, 2, 6), (3, 8, 4), (1, 8, 4), (2, 2, 6), (2, 8, 4),
)
PLACES = tuple(sum(block[2] for block in BLOCKS[:k]) for k in range(len(BLOCKS)))


def kernel(
    ids_hbm, row_hbm, counts_hbm, pivots, lower, upper, own_hbm, inner, factor, out,
    ids, ids_row, twin_row, counts, own_pivots,
    inverses, low, up, fac, chain, twin, link, mine, x_wide, y_wide, x_part, y_part, x_thin, y_thin,
    stack, column, work, bench,
    small_load, pivot_load, block_load, gather_send, gather_recv, inner_store, factor_store,
    twin_send, twin_recv, row_send, row_recv, send, recv, z_send, z_recv, q_send, q_recv,
):
    row, x = lax.axis_index("rows"), lax.axis_index("cols")
    core = lax.rem(row, CORES)
    z = lax.rem(lax.div(row, CORES), DEPTH)
    y = lax.div(row, CORES * DEPTH)
    count, size = pivots.shape[0], pivots.shape[-1]
    couplings, spots = counts.shape[0], mine.shape[3]
    group = PIECES[1][1]

    def device(x_at, y_at, z_at, core_at):
        return {"rows": (y_at * DEPTH + z_at) * CORES + core_at, "cols": x_at}

    sibling = device(x, y, z, 1 - core)
    along_x = lambda at: device(at, y, z, core)
    along_y = lambda at: device(x, at, z, core)
    along_z = lambda at: device(x, y, at, core)

    barrier = pltpu.get_barrier_semaphore()
    greeted = [sibling]
    greeted += [along_x(lax.rem(x + t, RING)) for t in (1, 2, 3)]
    greeted += [along_y(lax.rem(y + t, RING)) for t in (1, 3)]
    greeted += [along_z(lax.rem(z + t, DEPTH)) for t in range(1, DEPTH)]
    for peer in greeted:
        pl.semaphore_signal(barrier, inc=1, device_id=peer, device_id_type=pl.DeviceIdType.MESH)

    def source(offset):
        return lax.rem(x + offset, RING)

    small = [
        pltpu.make_async_copy(source_ref, into, small_load.at[k])
        for k, (source_ref, into) in enumerate(
            ((ids_hbm, ids), (row_hbm, ids_row), (counts_hbm, counts), (own_hbm, own_pivots))
        )
    ]

    def load_blocks(offset):
        members = pl.ds(source(offset) * count, count)
        return (
            pltpu.make_async_copy(lower.at[members, 0], low.at[members], block_load.at[0, offset]),
            pltpu.make_async_copy(upper.at[members, 0], up.at[members], block_load.at[1, offset]),
        )

    load_pivots = pltpu.make_async_copy(pivots, inverses.at[x], pivot_load)
    load_pivots.start()
    for copy in small:
        copy.start()
    pl.semaphore_wait(barrier, len(greeted))

    def gather(kind, piece):
        first, length = PIECES[piece]
        first, length = ((first, length), (first, length), (first, length // 2), (first + length // 2, length // 2))[kind]
        block = inverses.at[source((0, 0, 3, 1)[kind]), pl.ds(first, length)]
        return pltpu.make_async_remote_copy(
            src_ref=block,
            dst_ref=block,
            send_sem=gather_send.at[kind, piece],
            recv_sem=gather_recv.at[kind, piece],
            device_id=along_x(source(1 if kind % 2 == 0 else 3)),
            device_id_type=pl.DeviceIdType.MESH,
        )

    def pass_on(piece):
        for kind in (0, 1):
            gather(kind, piece).wait_recv()
            gather(kind + 2, piece).start()

    load_pivots.wait()
    gather(0, 0).start()
    gather(1, 0).start()
    for offset in range(RING):
        for copy in load_blocks(offset):
            copy.start()
    send_row = pltpu.make_async_remote_copy(
        src_ref=row_hbm, dst_ref=twin_row, send_sem=row_send, recv_sem=row_recv,
        device_id=sibling, device_id_type=pl.DeviceIdType.MESH,
    )
    send_row.start()

    def make_inverses(g, carry):
        @pl.when(g == 1)
        def _():
            for kind in (0, 1):
                gather(kind, 0).wait_send()

        @pl.when(g == 2)
        def _():
            for kind in (2, 3):
                gather(kind, 0).wait_recv()
                gather(kind, 0).wait_send()

        spots_of = []
        for b in range(group):
            at = source(jnp.where(g == 2, (3, 1, 2)[b % 3], 0))
            spots_of.append((at, jnp.where(g == 2, b // 3, lax.rem(RAW + g * group + b, count))))
            bench[b] = inverses[spots_of[b]]
        invert([bench.at[b] for b in range(group)], 16, eliminate_by_tile)
        for b in range(group):
            inverses[spots_of[b]] = bench[b]

        @pl.when(g == 0)
        def _():
            pass_on(0)
            gather(0, 1).start()
            gather(1, 1).start()

        @pl.when(g == 1)
        def _():
            gather(0, 2).start()
            gather(1, 2).start()

        return carry

    lax.fori_loop(0, 3, make_inverses, 0)
    store_inner = pltpu.make_async_copy(inverses.at[x], inner, inner_store)
    store_inner.start()
    pass_on(1)
    for copy in small:
        copy.wait()
    send_row.wait_recv()

    lane = lax.broadcasted_iota(jnp.int32, (1, couplings), 1)
    owner, local = lax.div(lane, count), lax.rem(lane, count)
    behind = lax.rem(owner + RING - x, RING)
    place = jnp.zeros_like(lane)
    for (offset, first, length), place_first in zip(BLOCKS, PLACES):
        here = (behind == offset) & (local >= first) & (local < first + length)
        place = jnp.where(here, local + (place_first - first), place)

    def newest(named, target, limit):
        found = jnp.max(jnp.where((named == target) & (place < limit), place, -1))
        return jnp.where(found < 0, couplings, found)

    names, twin_names = ids_row[...], twin_row[...]
    for (offset, first, length), place_first in zip(BLOCKS, PLACES):
        for b in range(length):
            link[place_first + b] = newest(names, ids[source(offset) * count + first + b], place_first + b)

    def find_last(spot, carry):
        link[couplings + spot] = newest(names, spot * CORES + core, couplings)
        link[couplings + spots + spot] = newest(twin_names, spot * CORES + core, couplings)
        return carry

    lax.fori_loop(0, spots, find_last, 0, unroll=8)
    chain[couplings] = jnp.zeros((size, size), jnp.float32)
    twin[couplings] = jnp.zeros((size, size), jnp.float32)

    stores = []

    crossed = []

    def couple(block):
        offset, first, length = BLOCKS[block]
        base, place_first = source(offset) * count + first, PLACES[block]
        for b in range(length):
            i, n = base + b, place_first + b
            value = jnp.where(x < counts[i], dot(low[i], inverses[source(offset), first + b]), 0.0)
            fac[i] = value
            chain[n] = dot(value, up[i]) + chain[link[n]]
        members, places = pl.ds(base, length), pl.ds(place_first, length)
        copy = pltpu.make_async_copy(fac.at[members], factor.at[members, 0], factor_store.at[block])
        copy.start()
        stores.append(copy)
        copy = pltpu.make_async_remote_copy(
            src_ref=chain.at[places], dst_ref=twin.at[places],
            send_sem=twin_send.at[block], recv_sem=twin_recv.at[block],
            device_id=sibling, device_id_type=pl.DeviceIdType.MESH,
        )
        copy.start()
        crossed.append(copy)

    for offset in range(RING):
        for copy in load_blocks(offset):
            copy.wait()
    for block in range(6):
        couple(block)
    pass_on(2)
    couple(6)
    couple(7)
    for block, piece in ((8, 1), (9, 2)):
        gather(2, piece).wait_recv()
        gather(3, piece).wait_recv()
        couple(block)
    for copy in crossed:
        copy.wait_recv()

    def lay_out(spot, carry):
        value = chain[link[couplings + spot]] + twin[link[couplings + spots + spot]]
        for quarter in range(RING):
            for half in range(2):
                for way in range(2):
                    at = quarter * 32 + half * 16 + way * TILE
                    mine[half, way, quarter, spot] = value[at : at + TILE, :]
        return carry

    lax.fori_loop(0, spots, lay_out, 0, unroll=4)

    def keep_x(way, value):
        x_part[way] = value

    def keep_y(way, value):
        y_part[way] = value

    wide_x = Ring("x", along_x, x, lambda way, d: mine.at[0, way, d], keep_x, x_wide, send.at[0], recv.at[0])
    wide_y = Ring(
        "y", along_y, y, lambda way, d: mine.at[1, way, :, pl.ds(d * DEPTH, DEPTH)], keep_y, y_wide,
        send.at[1], recv.at[1],
    )
    for stage in ("first", "second", "third"):
        getattr(wide_x, stage)()
        getattr(wide_y, stage)()

    def stack_x(way, value):
        for t in range(DEPTH):
            stack[t, way] = value[t]

    def stack_y(way, value):
        for t in range(DEPTH):
            stack[t, 2 + way] = value[t]

    thin_y = Ring(
        "y", along_y, y, lambda way, d: x_part.at[way, pl.ds(d * DEPTH, DEPTH)], stack_x, y_thin,
        send.at[2], recv.at[2],
    )
    thin_x = Ring("x", along_x, x, lambda way, d: y_part.at[way, d], stack_y, x_thin, send.at[3], recv.at[3])
    for stage in ("first", "second", "third"):
        getattr(thin_y, stage)()
        getattr(thin_x, stage)()

    spread = []
    for t in range(1, DEPTH):
        to = lax.rem(z + t, DEPTH)
        copy = pltpu.make_async_remote_copy(
            src_ref=stack.at[to],
            dst_ref=column.at[t - 1],
            send_sem=z_send.at[t - 1],
            recv_sem=z_recv.at[t - 1],
            device_id=along_z(to),
            device_id_type=pl.DeviceIdType.MESH,
        )
        copy.start()
        spread.append(copy)
    total = stack[z]
    for t in range(1, DEPTH):
        spread[t - 1].wait_recv()
        total = total + column[t - 1]

    rows = own_pivots.shape[0]
    work[x] = own_pivots[...] - total.reshape(rows, total.shape[-1])
    quarters = []
    for t in range(1, RING):
        copy = pltpu.make_async_remote_copy(
            src_ref=work.at[x],
            dst_ref=work.at[x],
            send_sem=q_send.at[t - 1],
            recv_sem=q_recv.at[t - 1],
            device_id=along_x(lax.rem(x + t, RING)),
            device_id_type=pl.DeviceIdType.MESH,
        )
        copy.start()
        quarters.append(copy)
    for copy in quarters:
        copy.wait()
    for ring in (wide_x, wide_y, thin_x, thin_y):
        ring.drain()
    for copy in crossed + spread:
        copy.wait_send()

    out[...] = work[...].reshape(out.shape)
    for piece in range(1, len(PIECES)):
        for kind in range(4):
            gather(kind, piece).wait_send()
    send_row.wait_send()
    for copy in stores + [store_inner]:
        copy.wait()


def deliver(inner, factor, reduced, inner_out, factor_out, own_out, held_inner, held_factor, whole, load, store):
    part = factor.shape[0] // PARTS
    moves = [(inner, held_inner, inner_out)]
    for k in range(PARTS):
        members = pl.ds(k * part, part)
        moves.append((factor.at[members], held_factor.at[members], factor_out.at[members]))
    loads = [pltpu.make_async_copy(here, held, load.at[k]) for k, (here, held, _) in enumerate(moves)]
    stores = [pltpu.make_async_copy(held, there, store.at[k]) for k, (_, held, there) in enumerate(moves)]
    for copy in loads:
        copy.start()

    def store_all():
        for arrived, copy in zip(loads, stores):
            arrived.wait()
            copy.start()

    whole[...] = reduced[...]
    invert([whole], 32, functools.partial(eliminate, ahead=16), store_all)
    rows = own_out.shape[0]
    own_out[...] = whole[pl.ds(pl.multiple_of(lax.axis_index("cols") * rows, rows), rows), :]
    for copy in stores:
        copy.wait()


def shards(inner_pivots, lower_blocks, upper_blocks, separator_pivots, separator_ids, coupling_count):
    f32 = jnp.float32
    count, size = inner_pivots.shape[0], inner_pivots.shape[1]
    couplings = lower_blocks.shape[0]
    separators = separator_pivots.shape[0] * lax.axis_size("rows")
    rows = separator_pivots.shape[1]
    spots = separators // CORES
    tile = (TILE, size)
    block = (size, size)
    dma = pltpu.SemaphoreType.DMA
    vmem = lambda *shape: pltpu.VMEM(shape, f32)
    inner_inverse, lower_factor, reduced = pl.pallas_call(
        kernel,
        out_shape=[
            jax.ShapeDtypeStruct(inner_pivots.shape, f32),
            jax.ShapeDtypeStruct(lower_blocks.shape, f32),
            jax.ShapeDtypeStruct(block, f32),
        ],
        in_specs=[HBM] * 7,
        out_specs=[ANY, ANY, VMEM],
        scratch_shapes=[
            pltpu.SMEM((couplings,), jnp.int32),
            pltpu.VMEM((1, couplings), jnp.int32),
            pltpu.VMEM((1, couplings), jnp.int32),
            pltpu.SMEM((couplings,), jnp.int32),
            vmem(rows, size),
            vmem(RING, count, *block),
            vmem(couplings, *block),
            vmem(couplings, *block),
            vmem(couplings, *block),
            vmem(couplings + 1, *block),
            vmem(couplings + 1, *block),
            pltpu.SMEM((couplings + 2 * spots,), jnp.int32),
            vmem(2, 2, RING, spots, *tile),
            vmem(6, spots, *tile),
            vmem(6, RING, DEPTH, *tile),
            vmem(2, spots, *tile),
            vmem(2, RING, DEPTH, *tile),
            vmem(6, DEPTH, *tile),
            vmem(6, DEPTH, *tile),
            vmem(DEPTH, 4, *tile),
            vmem(DEPTH - 1, 4, *tile),
            vmem(RING, rows, size),
            vmem(PIECES[1][1], *block),
            dma((4,)),
            dma,
            dma((2, RING)),
            dma((4, len(PIECES))),
            dma((4, len(PIECES))),
            dma,
            dma((len(BLOCKS),)),
            dma((len(BLOCKS),)),
            dma((len(BLOCKS),)),
            dma,
            dma,
            dma((4, 6)),
            dma((4, 6)),
            dma((DEPTH - 1,)),
            dma((DEPTH - 1,)),
            dma((RING - 1,)),
            dma((RING - 1,)),
        ],
        compiler_params=pltpu.CompilerParams(vmem_limit_bytes=GRANT, collective_id=0, has_side_effects=True),
    )(
        separator_ids.reshape(-1),
        separator_ids.reshape(1, -1),
        coupling_count,
        inner_pivots,
        lower_blocks,
        upper_blocks,
        separator_pivots[0],
    )
    inner_inverse, lower_factor, own = pl.pallas_call(
        deliver,
        out_shape=[
            jax.ShapeDtypeStruct(inner_pivots.shape, f32),
            jax.ShapeDtypeStruct(lower_blocks.shape, f32),
            jax.ShapeDtypeStruct((rows, size), f32),
        ],
        in_specs=[ANY, ANY, VMEM],
        out_specs=[HBM, HBM, VMEM],
        scratch_shapes=[
            vmem(*inner_pivots.shape),
            vmem(*lower_blocks.shape),
            vmem(*block),
            dma((PARTS + 1,)),
            dma((PARTS + 1,)),
        ],
        compiler_params=pltpu.CompilerParams(vmem_limit_bytes=GRANT),
    )(inner_inverse, lower_factor, reduced)
    return inner_inverse, lower_factor, own[None]


def solution(mesh):
    placed = (
        P(("rows", "cols"), None, None),
        P("rows", "cols", None, None),
        P("rows", "cols", None, None),
        P("rows", "cols", None),
        P("rows", "cols"),
        P("rows"),
    )
    return jax.shard_map(
        shards,
        mesh=mesh,
        in_specs=placed,
        out_specs=(
            P(("rows", "cols"), None, None),
            P("rows", "cols", None, None),
            P("rows", "cols", None),
        ),
        check_vma=False,
    )
```

```python
import functools

import jax
import jax.numpy as jnp
from jax import lax
from jax.experimental import pallas as pl
from jax.experimental.pallas import tpu as pltpu
from jax.sharding import PartitionSpec as P

HIGH = lax.Precision.HIGH
VMEM = pl.BlockSpec(memory_space=pltpu.VMEM)
HBM = pl.BlockSpec(memory_space=pltpu.HBM)
ANY = pl.BlockSpec(memory_space=pl.ANY)
GRANT = 63 << 20
CORES, RING, DEPTH, TILE = 2, 4, 8, 8


def dot(a, b):
    return lax.dot_general(a, b, (((1,), (0,)), ((), ())), precision=HIGH, preferred_element_type=jnp.float32)


def eliminate(slabs, first, ahead):
    depth, width = slabs[0].shape
    lanes = lax.broadcasted_iota(jnp.int32, (1, width), 1)
    rows = lax.broadcasted_iota(jnp.int32, (depth, width), 0)
    for start in range(0, depth, ahead):
        base = first + start
        spread = [
            [jnp.broadcast_to(slab[:, base + t : base + t + 1], (depth, width)) for t in range(ahead)]
            for slab in slabs
        ]
        for t in range(ahead):
            k = start + t
            at_lane = (lanes == base + t).astype(jnp.float32)
            at_row = (rows == k).astype(jnp.float32)
            for index, slab in enumerate(slabs):
                columns = spread[index]
                inverse = 1.0 / columns[t][k : k + 1, :]
                pivot_row = (slab[k : k + 1, :] + at_lane) * inverse
                column = columns[t] - at_row
                for u in range(t + 1, ahead):
                    columns[u] = columns[u] - column * (columns[u][k : k + 1, :] * inverse)
                slabs[index] = slab - column * pivot_row
    return slabs


def eliminate_by_tile(slabs, first):
    depth, width = slabs[0].shape
    lanes = lax.broadcasted_iota(jnp.int32, (1, width), 1)
    rows = lax.broadcasted_iota(jnp.int32, (TILE, width), 0)
    tiles = [[slab[t : t + TILE, :] for t in range(0, depth, TILE)] for slab in slabs]
    for q in range(depth // TILE):
        base = first + q * TILE
        inside = (lanes >= base) & (lanes < base + TILE)
        for parts in tiles:
            spread = [
                [jnp.broadcast_to(part[:, base + t : base + t + 1], (TILE, width)) for t in range(TILE)]
                for part in parts
            ]
            pivot, columns = parts[q], spread[q]
            for t in range(TILE):
                at_lane = (lanes == base + t).astype(jnp.float32)
                at_row = (rows == t).astype(jnp.float32)
                inverse = 1.0 / columns[t][t : t + 1, :]
                pivot_row = (pivot[t : t + 1, :] + at_lane) * inverse
                column = columns[t] - at_row
                for u in range(t + 1, TILE):
                    columns[u] = columns[u] - column * (columns[u][t : t + 1, :] * inverse)
                pivot = pivot - column * pivot_row
            parts[q] = pivot
            for other in range(len(parts)):
                if other != q:
                    value = jnp.where(inside, 0.0, parts[other])
                    for t in range(TILE):
                        value = value - spread[other][t] * pivot[t : t + 1, :]
                    parts[other] = value
    return [jnp.concatenate(parts, axis=0) for parts in tiles]


def invert(refs, panel, eliminate_slabs, after_first=None):
    size = refs[0].shape[-1]
    lanes = lax.broadcasted_iota(jnp.int32, (1, size), 1)
    for first in range(0, size, panel):
        slabs = eliminate_slabs([ref[first : first + panel, :] for ref in refs], first)
        inside = (lanes >= first) & (lanes < first + panel)
        for ref, slab in zip(refs, slabs):
            whole = ref[...]
            update = dot(whole[:, first : first + panel], slab)
            ref[...] = jnp.where(inside, 0.0, whole) - update
            ref[first : first + panel, :] = slab
        if first == panel and after_first is not None:
            after_first()


class Ring:
    def __init__(self, axis, step, me, blocks, own, land, send, recv):
        self.blocks, self.own, self.land, self.send, self.recv = blocks, own, land, send, recv
        self.me, self.axis, self.step = me, axis, step
        self.sent = []

    def at(self, offset):
        return lax.rem(self.me + offset, RING)

    def copy(self, slot, source, offset):
        copy = pltpu.make_async_remote_copy(
            src_ref=source,
            dst_ref=self.land.at[slot],
            send_sem=self.send.at[slot],
            recv_sem=self.recv.at[slot],
            device_id=self.step(self.at(offset)),
            device_id_type=pl.DeviceIdType.MESH,
        )
        copy.start()
        self.sent.append(copy)
        return copy

    def first(self):
        self.relay_up = self.copy(0, self.blocks(1, self.at(2)), 1)
        self.relay_down = self.copy(1, self.blocks(0, self.at(2)), 3)
        self.last_up = self.copy(2, self.blocks(0, self.at(1)), 1)
        self.last_down = self.copy(3, self.blocks(1, self.at(3)), 3)

    def second(self):
        self.relay_up.wait_recv()
        block = self.blocks(1, self.at(1))
        block[...] = block[...] + self.land[0]
        self.sum_up = self.copy(4, block, 1)
        self.relay_down.wait_recv()
        block = self.blocks(0, self.at(3))
        block[...] = block[...] + self.land[1]
        self.sum_down = self.copy(5, block, 3)

    def third(self):
        self.last_up.wait_recv()
        self.sum_down.wait_recv()
        self.own(0, self.blocks(0, self.me)[...] + (self.land[2] + self.land[5]))
        self.last_down.wait_recv()
        self.sum_up.wait_recv()
        self.own(1, self.blocks(1, self.me)[...] + (self.land[3] + self.land[4]))

    def drain(self):
        for copy in self.sent:
            copy.wait_send()


RAW = 2
PARTS = 4
PIECES = ((0, RAW), (RAW, 6), (RAW + 6, 4))
BLOCKS = (
    (0, 0, 12), (3, 0, 2), (1, 0, 2), (2, 0, 2), (3, 2, 6), (1, 2, 6), (3, 8, 4), (1, 8, 4), (2, 2, 6), (2, 8, 4),
)
PLACES = tuple(sum(block[2] for block in BLOCKS[:k]) for k in range(len(BLOCKS)))


def kernel(
    ids_hbm, row_hbm, counts_hbm, pivots, lower, upper, own_hbm, inner, factor, out,
    ids, ids_row, twin_row, counts, own_pivots,
    inverses, low, up, fac, chain, twin, link, mine, x_wide, y_wide, x_part, y_part, x_thin, y_thin,
    stack, column, work, bench,
    small_load, pivot_load, block_load, gather_send, gather_recv, inner_store, factor_store,
    twin_send, twin_recv, row_send, row_recv, send, recv, z_send, z_recv, q_send, q_recv,
):
    row, x = lax.axis_index("rows"), lax.axis_index("cols")
    core = lax.rem(row, CORES)
    z = lax.rem(lax.div(row, CORES), DEPTH)
    y = lax.div(row, CORES * DEPTH)
    count, size = pivots.shape[0], pivots.shape[-1]
    couplings, spots = counts.shape[0], mine.shape[3]
    group = PIECES[1][1]

    def device(x_at, y_at, z_at, core_at):
        return {"rows": (y_at * DEPTH + z_at) * CORES + core_at, "cols": x_at}

    sibling = device(x, y, z, 1 - core)
    along_x = lambda at: device(at, y, z, core)
    along_y = lambda at: device(x, at, z, core)
    along_z = lambda at: device(x, y, at, core)

    barrier = pltpu.get_barrier_semaphore()
    greeted = [sibling]
    greeted += [along_x(lax.rem(x + t, RING)) for t in (1, 2, 3)]
    greeted += [along_y(lax.rem(y + t, RING)) for t in (1, 3)]
    greeted += [along_z(lax.rem(z + t, DEPTH)) for t in range(1, DEPTH)]
    for peer in greeted:
        pl.semaphore_signal(barrier, inc=1, device_id=peer, device_id_type=pl.DeviceIdType.MESH)

    def source(offset):
        return lax.rem(x + offset, RING)

    small = [
        pltpu.make_async_copy(source_ref, into, small_load.at[k])
        for k, (source_ref, into) in enumerate(
            ((ids_hbm, ids), (row_hbm, ids_row), (counts_hbm, counts), (own_hbm, own_pivots))
        )
    ]

    def load_blocks(offset):
        members = pl.ds(source(offset) * count, count)
        return (
            pltpu.make_async_copy(lower.at[members, 0], low.at[members], block_load.at[0, offset]),
            pltpu.make_async_copy(upper.at[members, 0], up.at[members], block_load.at[1, offset]),
        )

    load_pivots = pltpu.make_async_copy(pivots, inverses.at[x], pivot_load)
    load_pivots.start()
    for copy in small:
        copy.start()
    pl.semaphore_wait(barrier, len(greeted))

    def gather(kind, piece):
        first, length = PIECES[piece]
        first, length = ((first, length), (first, length), (first, length // 2), (first + length // 2, length // 2))[kind]
        block = inverses.at[source((0, 0, 3, 1)[kind]), pl.ds(first, length)]
        return pltpu.make_async_remote_copy(
            src_ref=block,
            dst_ref=block,
            send_sem=gather_send.at[kind, piece],
            recv_sem=gather_recv.at[kind, piece],
            device_id=along_x(source(1 if kind % 2 == 0 else 3)),
            device_id_type=pl.DeviceIdType.MESH,
        )

    def pass_on(piece):
        for kind in (0, 1):
            gather(kind, piece).wait_recv()
            gather(kind + 2, piece).start()

    load_pivots.wait()
    gather(0, 0).start()
    gather(1, 0).start()
    for offset in range(RING):
        for copy in load_blocks(offset):
            copy.start()
    send_row = pltpu.make_async_remote_copy(
        src_ref=row_hbm, dst_ref=twin_row, send_sem=row_send, recv_sem=row_recv,
        device_id=sibling, device_id_type=pl.DeviceIdType.MESH,
    )
    send_row.start()

    def make_inverses(g, carry):
        @pl.when(g == 1)
        def _():
            for kind in (0, 1):
                gather(kind, 0).wait_send()

        @pl.when(g == 2)
        def _():
            for kind in (2, 3):
                gather(kind, 0).wait_recv()
                gather(kind, 0).wait_send()

        spots_of = []
        for b in range(group):
            at = source(jnp.where(g == 2, (3, 1, 2)[b % 3], 0))
            spots_of.append((at, jnp.where(g == 2, b // 3, lax.rem(RAW + g * group + b, count))))
            bench[b] = inverses[spots_of[b]]
        invert([bench.at[b] for b in range(group)], 16, eliminate_by_tile)
        for b in range(group):
            inverses[spots_of[b]] = bench[b]

        @pl.when(g == 0)
        def _():
            pass_on(0)
            gather(0, 1).start()
            gather(1, 1).start()

        @pl.when(g == 1)
        def _():
            gather(0, 2).start()
            gather(1, 2).start()

        return carry

    lax.fori_loop(0, 3, make_inverses, 0)
    store_inner = pltpu.make_async_copy(inverses.at[x], inner, inner_store)
    store_inner.start()
    pass_on(1)
    for copy in small:
        copy.wait()
    send_row.wait_recv()

    lane = lax.broadcasted_iota(jnp.int32, (1, couplings), 1)
    owner, local = lax.div(lane, count), lax.rem(lane, count)
    behind = lax.rem(owner + RING - x, RING)
    place = jnp.zeros_like(lane)
    for (offset, first, length), place_first in zip(BLOCKS, PLACES):
        here = (behind == offset) & (local >= first) & (local < first + length)
        place = jnp.where(here, local + (place_first - first), place)

    def newest(named, target, limit):
        found = jnp.max(jnp.where((named == target) & (place < limit), place, -1))
        return jnp.where(found < 0, couplings, found)

    names, twin_names = ids_row[...], twin_row[...]
    for (offset, first, length), place_first in zip(BLOCKS, PLACES):
        for b in range(length):
            link[place_first + b] = newest(names, ids[source(offset) * count + first + b], place_first + b)

    def find_last(spot, carry):
        link[couplings + spot] = newest(names, spot * CORES + core, couplings)
        link[couplings + spots + spot] = newest(twin_names, spot * CORES + core, couplings)
        return carry

    lax.fori_loop(0, spots, find_last, 0, unroll=8)
    chain[couplings] = jnp.zeros((size, size), jnp.float32)
    twin[couplings] = jnp.zeros((size, size), jnp.float32)

    stores = []

    crossed = []

    def couple(block):
        offset, first, length = BLOCKS[block]
        base, place_first = source(offset) * count + first, PLACES[block]
        for b in range(length):
            i, n = base + b, place_first + b
            value = jnp.where(x < counts[i], dot(low[i], inverses[source(offset), first + b]), 0.0)
            fac[i] = value
            chain[n] = dot(value, up[i]) + chain[link[n]]
        members, places = pl.ds(base, length), pl.ds(place_first, length)
        copy = pltpu.make_async_copy(fac.at[members], factor.at[members, 0], factor_store.at[block])
        copy.start()
        stores.append(copy)
        copy = pltpu.make_async_remote_copy(
            src_ref=chain.at[places], dst_ref=twin.at[places],
            send_sem=twin_send.at[block], recv_sem=twin_recv.at[block],
            device_id=sibling, device_id_type=pl.DeviceIdType.MESH,
        )
        copy.start()
        crossed.append(copy)

    for offset in range(RING):
        for copy in load_blocks(offset):
            copy.wait()
    for block in range(6):
        couple(block)
    pass_on(2)
    couple(6)
    couple(7)
    for block, piece in ((8, 1), (9, 2)):
        gather(2, piece).wait_recv()
        gather(3, piece).wait_recv()
        couple(block)
    for copy in crossed:
        copy.wait_recv()

    def lay_out(spot, carry):
        value = chain[link[couplings + spot]] + twin[link[couplings + spots + spot]]
        for quarter in range(RING):
            for half in range(2):
                for way in range(2):
                    at = quarter * 32 + half * 16 + way * TILE
                    mine[half, way, quarter, spot] = value[at : at + TILE, :]
        return carry

    lax.fori_loop(0, spots, lay_out, 0, unroll=4)

    def keep_x(way, value):
        x_part[way] = value

    def keep_y(way, value):
        y_part[way] = value

    wide_x = Ring("x", along_x, x, lambda way, d: mine.at[0, way, d], keep_x, x_wide, send.at[0], recv.at[0])
    wide_y = Ring(
        "y", along_y, y, lambda way, d: mine.at[1, way, :, pl.ds(d * DEPTH, DEPTH)], keep_y, y_wide,
        send.at[1], recv.at[1],
    )
    for stage in ("first", "second", "third"):
        getattr(wide_x, stage)()
        getattr(wide_y, stage)()

    def stack_x(way, value):
        for t in range(DEPTH):
            stack[t, way] = value[t]

    def stack_y(way, value):
        for t in range(DEPTH):
            stack[t, 2 + way] = value[t]

    thin_y = Ring(
        "y", along_y, y, lambda way, d: x_part.at[way, pl.ds(d * DEPTH, DEPTH)], stack_x, y_thin,
        send.at[2], recv.at[2],
    )
    thin_x = Ring("x", along_x, x, lambda way, d: y_part.at[way, d], stack_y, x_thin, send.at[3], recv.at[3])
    for stage in ("first", "second", "third"):
        getattr(thin_y, stage)()
        getattr(thin_x, stage)()

    spread = []
    for t in range(1, DEPTH):
        to = lax.rem(z + t, DEPTH)
        copy = pltpu.make_async_remote_copy(
            src_ref=stack.at[to],
            dst_ref=column.at[t - 1],
            send_sem=z_send.at[t - 1],
            recv_sem=z_recv.at[t - 1],
            device_id=along_z(to),
            device_id_type=pl.DeviceIdType.MESH,
        )
        copy.start()
        spread.append(copy)
    total = stack[z]
    for t in range(1, DEPTH):
        spread[t - 1].wait_recv()
        total = total + column[t - 1]

    rows = own_pivots.shape[0]
    work[x] = own_pivots[...] - total.reshape(rows, total.shape[-1])
    quarters = []
    for t in range(1, RING):
        copy = pltpu.make_async_remote_copy(
            src_ref=work.at[x],
            dst_ref=work.at[x],
            send_sem=q_send.at[t - 1],
            recv_sem=q_recv.at[t - 1],
            device_id=along_x(lax.rem(x + t, RING)),
            device_id_type=pl.DeviceIdType.MESH,
        )
        copy.start()
        quarters.append(copy)
    for copy in quarters:
        copy.wait()
    for ring in (wide_x, wide_y, thin_x, thin_y):
        ring.drain()
    for copy in crossed + spread:
        copy.wait_send()

    out[...] = work[...].reshape(out.shape)
    for piece in range(1, len(PIECES)):
        for kind in range(4):
            gather(kind, piece).wait_send()
    send_row.wait_send()
    for copy in stores + [store_inner]:
        copy.wait()


def deliver(inner, factor, reduced, inner_out, factor_out, own_out, held_inner, held_factor, whole, load, store):
    part = factor.shape[0] // PARTS
    moves = [(inner, held_inner, inner_out)]
    for k in range(PARTS):
        members = pl.ds(k * part, part)
        moves.append((factor.at[members], held_factor.at[members], factor_out.at[members]))
    loads = [pltpu.make_async_copy(here, held, load.at[k]) for k, (here, held, _) in enumerate(moves)]
    stores = [pltpu.make_async_copy(held, there, store.at[k]) for k, (_, held, there) in enumerate(moves)]
    for copy in loads:
        copy.start()

    def store_all():
        for arrived, copy in zip(loads, stores):
            arrived.wait()
            copy.start()

    whole[...] = reduced[...]
    invert([whole], 32, functools.partial(eliminate, ahead=16), store_all)
    rows = own_out.shape[0]
    own_out[...] = whole[pl.ds(pl.multiple_of(lax.axis_index("cols") * rows, rows), rows), :]
    for copy in stores:
        copy.wait()


def shards(inner_pivots, lower_blocks, upper_blocks, separator_pivots, separator_ids, coupling_count):
    f32 = jnp.float32
    count, size = inner_pivots.shape[0], inner_pivots.shape[1]
    couplings = lower_blocks.shape[0]
    separators = separator_pivots.shape[0] * lax.axis_size("rows")
    rows = separator_pivots.shape[1]
    spots = separators // CORES
    tile = (TILE, size)
    block = (size, size)
    dma = pltpu.SemaphoreType.DMA
    vmem = lambda *shape: pltpu.VMEM(shape, f32)
    inner_inverse, lower_factor, reduced = pl.pallas_call(
        kernel,
        out_shape=[
            jax.ShapeDtypeStruct(inner_pivots.shape, f32),
            jax.ShapeDtypeStruct(lower_blocks.shape, f32),
            jax.ShapeDtypeStruct(block, f32),
        ],
        in_specs=[HBM] * 7,
        out_specs=[ANY, ANY, VMEM],
        scratch_shapes=[
            pltpu.SMEM((couplings,), jnp.int32),
            pltpu.VMEM((1, couplings), jnp.int32),
            pltpu.VMEM((1, couplings), jnp.int32),
            pltpu.SMEM((couplings,), jnp.int32),
            vmem(rows, size),
            vmem(RING, count, *block),
            vmem(couplings, *block),
            vmem(couplings, *block),
            vmem(couplings, *block),
            vmem(couplings + 1, *block),
            vmem(couplings + 1, *block),
            pltpu.SMEM((couplings + 2 * spots,), jnp.int32),
            vmem(2, 2, RING, spots, *tile),
            vmem(6, spots, *tile),
            vmem(6, RING, DEPTH, *tile),
            vmem(2, spots, *tile),
            vmem(2, RING, DEPTH, *tile),
            vmem(6, DEPTH, *tile),
            vmem(6, DEPTH, *tile),
            vmem(DEPTH, 4, *tile),
            vmem(DEPTH - 1, 4, *tile),
            vmem(RING, rows, size),
            vmem(PIECES[1][1], *block),
            dma((4,)),
            dma,
            dma((2, RING)),
            dma((4, len(PIECES))),
            dma((4, len(PIECES))),
            dma,
            dma((len(BLOCKS),)),
            dma((len(BLOCKS),)),
            dma((len(BLOCKS),)),
            dma,
            dma,
            dma((4, 6)),
            dma((4, 6)),
            dma((DEPTH - 1,)),
            dma((DEPTH - 1,)),
            dma((RING - 1,)),
            dma((RING - 1,)),
        ],
        compiler_params=pltpu.CompilerParams(vmem_limit_bytes=GRANT, collective_id=0, has_side_effects=True),
    )(
        separator_ids.reshape(-1),
        separator_ids.reshape(1, -1),
        coupling_count,
        inner_pivots,
        lower_blocks,
        upper_blocks,
        separator_pivots[0],
    )
    inner_inverse, lower_factor, own = pl.pallas_call(
        deliver,
        out_shape=[
            jax.ShapeDtypeStruct(inner_pivots.shape, f32),
            jax.ShapeDtypeStruct(lower_blocks.shape, f32),
            jax.ShapeDtypeStruct((rows, size), f32),
        ],
        in_specs=[ANY, ANY, VMEM],
        out_specs=[HBM, HBM, VMEM],
        scratch_shapes=[
            vmem(*inner_pivots.shape),
            vmem(*lower_blocks.shape),
            vmem(*block),
            dma((PARTS + 1,)),
            dma((PARTS + 1,)),
        ],
        compiler_params=pltpu.CompilerParams(vmem_limit_bytes=GRANT),
    )(inner_inverse, lower_factor, reduced)
    return inner_inverse, lower_factor, own[None]


def solution(mesh):
    placed = (
        P(("rows", "cols"), None, None),
        P("rows", "cols", None, None),
        P("rows", "cols", None, None),
        P("rows", "cols", None),
        P("rows", "cols"),
        P("rows"),
    )
    return jax.shard_map(
        shards,
        mesh=mesh,
        in_specs=placed,
        out_specs=(
            P(("rows", "cols"), None, None),
            P("rows", "cols", None, None),
            P("rows", "cols", None),
        ),
        check_vma=False,
    )
```
